32 devices in a mesh: groups: 2 (over y), ctx: 4 (over z), head: 4 (over x, core).
Axes of the slice: x: 2, y: 2, z: 4, core: 2. Of those that a mesh axis runs over, the one named last changes fastest.
Arguments:
- queries: bfloat16 [65536, 2048], P(('groups', 'ctx'), 'head'), parts along dimension 0, may hold values from -9 to 9
- keys: bfloat16 [65536, 1024], P(('groups', 'ctx'), 'head'), parts along dimension 0, may hold values from -6 to 6
- values: bfloat16 [65536, 1024], P(('groups', 'ctx'), 'head'), parts along dimension 0, may hold values from -6 to 6
- doc_lengths: int32 [32], P('groups'), parts along dimension 0, may hold values from 1 to 8192, 32768 in all
- live_blocks: int32 [8], P('groups'), parts along dimension 0, may hold values from 1 to 16, as said below
Outputs:
- attended: bfloat16 [65536, 2048], P(('groups', 'ctx'), 'head'), parts along dimension 0
- log_norm: float32 [32, 32768], P(('groups', 'head'), 'ctx'), parts along dimension 0
The draws below stay inside these ranges and needn't reach their ends.
There are 2 independent parts, one for each index of `groups`. The reference program is written for one: setup_inputs(seed, part) draws one part's arguments, and reference() takes and returns one part's arrays. A program takes and returns all parts, laid end to end along the dimension named above; each array names one. Nothing has to cross between parts.
Inputs may be any that keep to these rules, and one draw needn't show every extreme that they name: `live_blocks`: shards are paired heavy with light: for every shard s below 2, one of shards s and s + 2 has 16 scored blocks and the other fewer than 16.
All inputs are finite; a program needn't handle non-finite values.
Results may differ from the reference program's by a relative error of at most 0.0043.
Values may be sent and summed in bfloat16 or wider, within the bound.
A program may use at most 128 MiB of HBM per device.

```python
import math
import jax
import jax.numpy as jnp
import numpy as np
from jax import lax

HD = 128
QH = 16
KVH = 8
W = 1024
BLK = 512
DOCS = 16
SEQ_DEV = 8192
SEQ = 32768
NBLK = 16
SHARDS = 4


def query_key_pair(key):
    base = jax.random.fold_in(key, 11)
    key_query, key_keys = jax.random.split(base, 2)
    query_vals = jnp.clip(jax.random.normal(key_query, (SEQ, QH * HD), jnp.float32), -6.0, 6.0)
    key_vals = jnp.clip(jax.random.normal(key_keys, (SEQ, KVH * HD), jnp.float32), -6.0, 6.0)
    return (query_vals, key_vals)


def draw_queries(key, part):
    query_vals, key_vals = query_key_pair(key)
    return query_vals.astype(jnp.bfloat16)


def draw_keys(key, part):
    query_vals, key_vals = query_key_pair(key)
    return key_vals.astype(jnp.bfloat16)


def draw_live_blocks(key, part):
    key_side = jax.random.fold_in(key, 5)
    key_light = jax.random.fold_in(key, 6)
    half_shards = SHARDS // 2
    low_heavy = jax.random.randint(key_side, (half_shards,), 0, 2) == 0
    light_counts = jax.random.randint(key_light, (half_shards,), 1, NBLK)
    low_counts = jnp.where(low_heavy, NBLK, light_counts)
    high_counts = jnp.where(low_heavy, light_counts, NBLK)
    return jnp.concatenate([low_counts, high_counts]).astype(jnp.int32)


def level_of(stream_key, shape, cuts, smallest, top_value):
    level = 1.0
    for position, shards_of in cuts:
        heights = jax.random.uniform(jax.random.fold_in(jax.random.fold_in(stream_key, 6), position), (shards_of,), jnp.float32, smallest / len(cuts), top_value / len(cuts))
        level = level * jnp.repeat(jnp.exp(heights), shape[position] // shards_of).reshape((-1,) + (1,) * (len(shape) - 1 - position))
    return level


def length_profile(count, total, bound, skew):
    portions = [(1 << 20) // math.isqrt(standing ** skew) + 1 for standing in range(2, count + 1)]
    spare, given = total - bound - (count - 1), [1] * (count - 1)
    while spare > 0:
        candidates = [i for i in range(count - 1) if given[i] < bound]
        mass, left = sum([portions[i] for i in candidates]), spare
        for i in candidates:
            extra = min(bound - given[i], max(1, left * portions[i] // mass), spare)
            given[i] = given[i] + extra
            spare = spare - extra
    return np.array([bound] + given)


def uneven(key, count, total, reach, slope):
    if count == 2:
        one = jax.random.randint(key, (), max(1, total - reach), min(reach, total - 1) + 1)
        return jnp.stack([one, total - one])
    sizes = jnp.asarray(length_profile(count, total, reach, slope), jnp.int32)
    couples = (count - 1) // 2
    giver, receiver = sizes[1:1 + 2 * couples:2], sizes[2:2 + 2 * couples:2]
    margin = jnp.minimum(giver - 1, reach - receiver)
    moved = jax.random.randint(jax.random.fold_in(key, 1), (couples,), 0, 1 << 20) % (margin + 1)
    sizes = sizes.at[1:1 + 2 * couples:2].set(giver - moved).at[2:2 + 2 * couples:2].set(receiver + moved)
    return sizes[jax.random.permutation(jax.random.fold_in(key, 2), count)]


def bell_draw(key, dims, scale, bound, shards=(), held_as=jnp.bfloat16):
    gain = level_of(key, dims, shards, -0.22, 0.18) if shards else 1.0
    values = jax.random.normal(key, dims, jnp.float32) * scale * gain
    return jnp.minimum(jnp.maximum(values, -bound), bound).astype(held_as)


def setup_inputs(seed: int = 0, part: int = 0) -> dict:
    arg_keys = jax.random.split(jax.random.key(seed), 6)
    part_keys = jax.random.split(jax.random.fold_in(arg_keys[5], part), 6)
    queries = draw_queries(jax.random.fold_in(jax.random.fold_in(arg_keys[5], part), 71), part)
    keys = draw_keys(jax.random.fold_in(jax.random.fold_in(arg_keys[5], part), 71), part)
    values = bell_draw(part_keys[2], (SEQ, KVH * HD), 1.0, 6.0, ((0, 4), (1, 4)))
    doc_lengths = uneven(part_keys[3], DOCS, SEQ, SEQ // 4, 2).astype(jnp.int32)
    live_blocks = draw_live_blocks(jax.random.fold_in(jax.random.fold_in(arg_keys[5], part), 71), part)
    return {"queries": queries, "keys": keys, "values": values, "doc_lengths": doc_lengths, "live_blocks": live_blocks}


score_scale = 168.0 ** -0.5


def doc_index(starts, positions):
    return jnp.sum((starts[None, :] <= positions[:, None]).astype(jnp.int32), axis=1) - 1


def reference(queries, keys, values, doc_lengths, live_blocks):
    starts = (jnp.cumsum(doc_lengths) - doc_lengths).astype(jnp.int32)
    zero_rows = jnp.zeros((W, KVH * HD), keys.dtype)
    keys_pad = jnp.concatenate([zero_rows, keys], axis=0)
    values_pad = jnp.concatenate([zero_rows, values], axis=0)
    span = W + BLK

    def one_block(block_idx):
        row_start = (block_idx * BLK).astype(jnp.int32)
        shard_id = row_start // SEQ_DEV
        local_block = (row_start % SEQ_DEV) // BLK
        alive = local_block < live_blocks[shard_id]

        def compute(unused):
            query_blk = lax.dynamic_slice_in_dim(queries, row_start, BLK, 0).astype(jnp.float32).reshape(BLK, KVH, 2, HD)
            key_blk = lax.dynamic_slice_in_dim(keys_pad, row_start, span, 0).astype(jnp.float32).reshape(span, KVH, HD)
            value_blk = lax.dynamic_slice_in_dim(values_pad, row_start, span, 0).astype(jnp.float32).reshape(span, KVH, HD)
            scores = jnp.einsum("qhgd,khd->hgqk", query_blk, key_blk) * score_scale
            query_pos = row_start + jnp.arange(BLK, dtype=jnp.int32)
            key_pos = row_start - W + jnp.arange(span, dtype=jnp.int32)
            allowed = (doc_index(starts, key_pos)[None, :] == doc_index(starts, query_pos)[:, None])
            allowed = allowed & (key_pos[None, :] <= query_pos[:, None]) & (key_pos[None, :] > query_pos[:, None] - W) & (key_pos[None, :] >= 0)
            allowed = allowed[None, None]
            top = jnp.max(jnp.where(allowed, scores, -jnp.inf), axis=-1, keepdims=True)
            probs = jnp.where(allowed, jnp.exp(scores - top), 0.0)
            total = jnp.sum(probs, axis=-1)
            weights = lax.optimization_barrier(probs.astype(jnp.bfloat16)).astype(jnp.float32)
            mixed = jnp.einsum("hgqk,khd->qhgd", weights, value_blk) / jnp.transpose(total, (2, 0, 1))[..., None]
            attended = mixed.astype(jnp.bfloat16).reshape(BLK, QH * HD)
            log_norm = (top[..., 0] + jnp.log(total)).reshape(QH, BLK)
            return attended, log_norm

        def empty(unused):
            return jnp.zeros((BLK, QH * HD), jnp.bfloat16), jnp.zeros((QH, BLK), jnp.float32)

        return lax.cond(alive, compute, empty, 0)

    attended, log_norm = lax.map(one_block, jnp.arange(SEQ // BLK, dtype=jnp.int32))
    return attended.reshape(SEQ, QH * HD), jnp.transpose(log_norm, (1, 0, 2)).reshape(QH, SEQ)
```

```python
import math

import jax
import jax.numpy as jnp
from jax import lax
from jax.experimental import pallas as pl
from jax.experimental.pallas import tpu as pltpu
from jax.sharding import PartitionSpec as P

HD = 128
W = 1024
BLK = 512
QT = 256
KT = 256
SPAN = W + BLK
TILES = (W + QT) // KT
SCALE = 168.0 ** (-0.5)
SCALE2 = SCALE * math.log2(math.e)
TOTAL_LO = 2.0 ** -40
TOTAL_HI = 2.0 ** 100


def from_behind(shard, axis, by):
    devices = lax.axis_size(axis)
    pairs = [(i, i + by) for i in range(devices) if 0 <= i + by < devices]
    return lax.ppermute(shard, axis, pairs)


def doc_start(lengths_ref, position):
    start = jnp.int32(0)
    found = jnp.int32(0)
    for n in range(lengths_ref.shape[0]):
        found = jnp.where(start <= position, start, found)
        start = start + lengths_ref[n]
    return found


def scores_of(q2, k_ref, row, g):
    k = k_ref[pl.ds(row, KT), g * HD : (g + 1) * HD]
    return lax.dot_general(q2, k, (((1,), (1,)), ((), ())), preferred_element_type=jnp.float32)


def mix(p, v_ref, row, g):
    v = v_ref[pl.ds(row, KT), g * HD : (g + 1) * HD]
    v_ones = jnp.concatenate([v, jnp.ones((KT, HD), v.dtype)], axis=1)
    return jnp.dot(p, v_ones, preferred_element_type=jnp.float32)


def stacked_queries(q_ref, r0, g):
    a = q_ref[pl.ds(r0, QT), 2 * g * HD : (2 * g + 1) * HD]
    b = q_ref[pl.ds(r0, QT), (2 * g + 1) * HD : (2 * g + 2) * HD]
    return jnp.concatenate([a, b], axis=0)


def finish(acc, g, r0, o_ref, n_ref, range_ref, top=None):
    total = acc[:, HD:]
    out = (acc[:, :HD] / total).astype(o_ref.dtype)
    for h in range(2):
        col = (2 * g + h) * HD
        o_ref[pl.ds(r0, QT), col : col + HD] = out[h * QT : (h + 1) * QT]
        row = jnp.log(jnp.transpose(total[h * QT : (h + 1) * QT])[0:1, :])
        if top is not None:
            row = row + jnp.transpose(top[h * QT : (h + 1) * QT])[0:1, :] * SCALE
        n_ref[2 * g + h : 2 * g + h + 1, pl.ds(r0, QT)] = row
    if top is None:
        folded = total.reshape(2 * QT // 8, 8, HD)
        range_ref[0] = jnp.minimum(range_ref[0], jnp.min(folded, axis=0))
        range_ref[1] = jnp.maximum(range_ref[1], jnp.max(folded, axis=0))


def set_low(lengths_ref, lo_ref, q0):
    q = lax.broadcasted_iota(jnp.int32, (QT, HD), 0)
    low = q + 1
    start = jnp.int32(0)
    first = q0 - W
    lo_ref[...] = low
    for n in range(lengths_ref.shape[0]):
        here = start

        @pl.when((here > first) & (here < q0 + QT))
        def _():
            rel = here - first
            at = lax.broadcasted_iota(jnp.int32, (QT, HD), 0) + W
            lo_ref[...] = jnp.where(at >= rel, jnp.maximum(lo_ref[...], rel), lo_ref[...])

        start = start + lengths_ref[n]


def tile_mask(lo_ref, j):
    key = lax.broadcasted_iota(jnp.int32, (QT, KT), 1) + j * KT
    query = lax.broadcasted_iota(jnp.int32, (QT, KT), 0) + W
    low = lo_ref[...]
    low = jnp.concatenate([low] * (KT // HD), axis=1)
    return (key >= low) & (key <= query)


def masked(mask, x, other):
    return jnp.where(mask[None], x.reshape(2, QT, KT), other).reshape(2 * QT, KT)


def attend_clean(r0, groups, q_ref, k_ref, v_ref, o_ref, n_ref, range_ref):
    row = lax.broadcasted_iota(jnp.int32, (QT, KT), 0)
    col = lax.broadcasted_iota(jnp.int32, (QT, KT), 1)
    edge = col > row
    for g in range(groups):
        q2 = stacked_queries(q_ref, r0, g)
        first, last = r0, r0 + (TILES - 1) * KT
        p = jnp.exp2(
            masked(edge, scores_of(q2, k_ref, first, g), scores_of(q2, k_ref, last, g).reshape(2, QT, KT))
            * SCALE2
        )
        acc = mix(masked(edge, p, 0.0).astype(jnp.bfloat16), v_ref, first, g)
        acc += mix(masked(~edge, p, 0.0).astype(jnp.bfloat16), v_ref, last, g)
        for j in range(1, TILES - 1):
            p = jnp.exp2(scores_of(q2, k_ref, r0 + j * KT, g) * SCALE2)
            acc += mix(p.astype(jnp.bfloat16), v_ref, r0 + j * KT, g)
        finish(acc, g, r0, o_ref, n_ref, range_ref)


def attend_masked(r0, j_lo, groups, q_ref, k_ref, v_ref, o_ref, n_ref, range_ref, lo_ref, acc_ref):
    acc_ref[...] = jnp.zeros_like(acc_ref)

    @pl.loop(j_lo, TILES)
    def _(j):
        mask = tile_mask(lo_ref, j)
        row = pl.multiple_of(r0 + j * KT, KT)
        for g in range(groups):
            q2 = stacked_queries(q_ref, r0, g)
            p = masked(mask, jnp.exp2(scores_of(q2, k_ref, row, g) * SCALE2), 0.0)
            acc_ref[g] += mix(p.astype(jnp.bfloat16), v_ref, row, g)

    for g in range(groups):
        finish(acc_ref[g], g, r0, o_ref, n_ref, range_ref)


def attend_shifted(r0, j_lo, groups, q_ref, k_ref, v_ref, o_ref, n_ref, range_ref, lo_ref, acc_ref, top_ref):
    for g in range(groups):
        top_ref[...] = jnp.full_like(top_ref, -jnp.inf)
        acc_ref[g] = jnp.zeros_like(acc_ref[g])

        @pl.loop(j_lo, TILES)
        def _(j):
            row = pl.multiple_of(r0 + j * KT, KT)
            q2 = stacked_queries(q_ref, r0, g)
            s = masked(tile_mask(lo_ref, j), scores_of(q2, k_ref, row, g), -jnp.inf)
            top_ref[...] = jnp.maximum(top_ref[...], jnp.max(s, axis=1, keepdims=True))

        @pl.loop(j_lo, TILES)
        def _(j):
            row = pl.multiple_of(r0 + j * KT, KT)
            q2 = stacked_queries(q_ref, r0, g)
            top = jnp.concatenate([top_ref[...]] * (KT // HD), axis=1)
            p = jnp.exp2((scores_of(q2, k_ref, row, g) - top) * SCALE2)
            p = masked(tile_mask(lo_ref, j), p, 0.0)
            acc_ref[g] += mix(p.astype(jnp.bfloat16), v_ref, row, g)

        finish(acc_ref[g], g, r0, o_ref, n_ref, range_ref, top_ref[...])


def block_kernel(
    first_block, shard_rows, aliased, lengths_ref, live_ref, q_ref, k_ref, v_ref, *rest
):
    rest = rest[2:] if aliased else rest
    o_ref, n_ref, range_ref, lo_ref, acc_ref, top_ref = rest
    groups = k_ref.shape[1] // HD
    shard = lax.axis_index("ctx")
    block = pl.program_id(0) + first_block
    alive = block < live_ref[shard]
    block_start = shard * shard_rows + block * BLK

    @pl.when(jnp.logical_not(alive))
    def _():
        o_ref[...] = jnp.zeros_like(o_ref)
        n_ref[...] = jnp.zeros_like(n_ref)

    @pl.when(alive)
    def _():
        range_ref[0] = jnp.full((8, HD), TOTAL_HI, jnp.float32)
        range_ref[1] = jnp.full((8, HD), TOTAL_LO, jnp.float32)
        refs = (q_ref, k_ref, v_ref, o_ref, n_ref, range_ref)

        def low_tile(q0):
            reach = doc_start(lengths_ref, q0) - (q0 - W)
            return jnp.clip(reach // KT, 0, TILES - 1)

        @pl.loop(0, BLK // QT)
        def _(t):
            r0 = pl.multiple_of(t * QT, QT)
            q0 = block_start + r0
            clean = doc_start(lengths_ref, q0 + QT - 1) <= q0 - W + 1

            @pl.when(clean)
            def _():
                attend_clean(r0, groups, *refs)

            @pl.when(jnp.logical_not(clean))
            def _():
                set_low(lengths_ref, lo_ref, q0)
                attend_masked(r0, low_tile(q0), groups, *refs, lo_ref, acc_ref)

        in_range = (jnp.min(range_ref[0]) >= TOTAL_LO) & (jnp.max(range_ref[1]) <= TOTAL_HI)

        @pl.when(jnp.logical_not(in_range))
        def _():
            @pl.loop(0, BLK // QT)
            def _(t):
                r0 = pl.multiple_of(t * QT, QT)
                q0 = block_start + r0
                set_low(lengths_ref, lo_ref, q0)
                attend_shifted(r0, low_tile(q0), groups, *refs, lo_ref, acc_ref, top_ref)


def run_blocks(first_block, blocks, lengths, live, queries, keys, values, carried=None):
    shard_rows, width = queries.shape
    kv_width = keys.shape[1]
    heads = width // HD
    groups = kv_width // HD
    aliased = carried is not None

    def kernel(*refs):
        block_kernel(first_block, shard_rows, aliased, *refs)

    in_specs = [
        pl.BlockSpec((BLK, width), lambda i, *_: (i + first_block, 0)),
        pl.BlockSpec((pl.Element(SPAN), pl.Element(kv_width)), lambda i, *_: (i * BLK, 0)),
        pl.BlockSpec((pl.Element(SPAN), pl.Element(kv_width)), lambda i, *_: (i * BLK, 0)),
    ]
    if aliased:
        in_specs += [pl.BlockSpec(memory_space=pl.ANY)] * 2
    pairs = blocks * BLK * W * heads
    return pl.pallas_call(
        kernel,
        out_shape=(
            jax.ShapeDtypeStruct((shard_rows, width), jnp.bfloat16),
            jax.ShapeDtypeStruct((heads, shard_rows), jnp.float32),
        ),
        grid_spec=pltpu.PrefetchScalarGridSpec(
            num_scalar_prefetch=2,
            grid=(blocks,),
            in_specs=in_specs,
            out_specs=(
                pl.BlockSpec((BLK, width), lambda i, *_: (i + first_block, 0)),
                pl.BlockSpec((heads, BLK), lambda i, *_: (0, i + first_block)),
            ),
            scratch_shapes=[
                pltpu.VMEM((2, 8, HD), jnp.float32),
                pltpu.VMEM((QT, HD), jnp.int32),
                pltpu.VMEM((groups, 2 * QT, 2 * HD), jnp.float32),
                pltpu.VMEM((2 * QT, HD), jnp.float32),
            ],
        ),
        input_output_aliases={5: 0, 6: 1} if aliased else {},
        compiler_params=pltpu.CompilerParams(vmem_limit_bytes=48 << 20),
        cost_estimate=pl.CostEstimate(
            flops=4 * pairs * HD,
            transcendentals=pairs,
            bytes_accessed=blocks * (4 * BLK * width + 4 * SPAN * kv_width),
        ),
    )(lengths, live, queries, keys, values, *(carried or ()))


def local(queries, keys, values, doc_lengths, live_blocks):
    shard_rows = queries.shape[0]
    halo_blocks = W // BLK
    prev_keys, prev_values = from_behind(
        (keys[shard_rows - W :], values[shard_rows - W :]), "ctx", 1
    )
    done = run_blocks(
        halo_blocks, shard_rows // BLK - halo_blocks, doc_lengths, live_blocks, queries, keys, values
    )
    head_keys = jnp.concatenate([prev_keys, keys[:W]], axis=0)
    head_values = jnp.concatenate([prev_values, values[:W]], axis=0)
    return run_blocks(
        0, halo_blocks, doc_lengths, live_blocks, queries, head_keys, head_values, done
    )


def solution(mesh):
    in_specs = (
        P(("groups", "ctx"), "head"),
        P(("groups", "ctx"), "head"),
        P(("groups", "ctx"), "head"),
        P("groups"),
        P("groups"),
    )
    out_specs = (P(("groups", "ctx"), "head"), P(("groups", "head"), "ctx"))
    return jax.shard_map(local, mesh=mesh, in_specs=in_specs, out_specs=out_specs, check_vma=False)
```

```python
import math

import jax
import jax.numpy as jnp
from jax import lax
from jax.experimental import pallas as pl
from jax.experimental.pallas import tpu as pltpu
from jax.sharding import PartitionSpec as P

HD = 128
W = 1024
BLK = 512
QT = 256
KT = 256
SPAN = W + BLK
TILES = (W + QT) // KT
SCALE = 168.0 ** (-0.5)
SCALE2 = SCALE * math.log2(math.e)
TOTAL_LO = 2.0 ** -40
TOTAL_HI = 2.0 ** 100


def from_behind(shard, axis, by):
    devices = lax.axis_size(axis)
    pairs = [(i, i + by) for i in range(devices) if 0 <= i + by < devices]
    return lax.ppermute(shard, axis, pairs)


def doc_start(lengths_ref, position):
    start = jnp.int32(0)
    found = jnp.int32(0)
    for n in range(lengths_ref.shape[0]):
        found = jnp.where(start <= position, start, found)
        start = start + lengths_ref[n]
    return found


def scores_of(q2, k_ref, row, g, count=1):
    k = k_ref[pl.ds(row, count * KT), g * HD : (g + 1) * HD]
    return lax.dot_general(q2, k, (((1,), (1,)), ((), ())), preferred_element_type=jnp.float32)


def mix(p, v_ref, row, g, count=1):
    v = v_ref[pl.ds(row, count * KT), g * HD : (g + 1) * HD]
    v_ones = jnp.concatenate([v, jnp.ones((count * KT, HD), v.dtype)], axis=1)
    return jnp.dot(p, v_ones, preferred_element_type=jnp.float32)


def stacked_queries(q_ref, r0, g):
    a = q_ref[pl.ds(r0, QT), 2 * g * HD : (2 * g + 1) * HD]
    b = q_ref[pl.ds(r0, QT), (2 * g + 1) * HD : (2 * g + 2) * HD]
    return jnp.concatenate([a, b], axis=0)


def finish(acc, g, r0, o_ref, n_ref, range_ref, top=None):
    total = acc[:, HD:]
    out = (acc[:, :HD] / total).astype(o_ref.dtype)
    for h in range(2):
        col = (2 * g + h) * HD
        o_ref[pl.ds(r0, QT), col : col + HD] = out[h * QT : (h + 1) * QT]
        row = jnp.log(jnp.transpose(total[h * QT : (h + 1) * QT])[0:1, :])
        if top is not None:
            row = row + jnp.transpose(top[h * QT : (h + 1) * QT])[0:1, :] * SCALE
        n_ref[2 * g + h : 2 * g + h + 1, pl.ds(r0, QT)] = row
    if top is None:
        folded = total.reshape(2 * QT // 8, 8, HD)
        range_ref[0] = jnp.minimum(range_ref[0], jnp.min(folded, axis=0))
        range_ref[1] = jnp.maximum(range_ref[1], jnp.max(folded, axis=0))


def set_low(lengths_ref, lo_ref, q0):
    q = lax.broadcasted_iota(jnp.int32, (QT, HD), 0)
    low = q + 1
    start = jnp.int32(0)
    first = q0 - W
    lo_ref[...] = low
    for n in range(lengths_ref.shape[0]):
        here = start

        @pl.when((here > first) & (here < q0 + QT))
        def _():
            rel = here - first
            at = lax.broadcasted_iota(jnp.int32, (QT, HD), 0) + W
            lo_ref[...] = jnp.where(at >= rel, jnp.maximum(lo_ref[...], rel), lo_ref[...])

        start = start + lengths_ref[n]


def tile_mask(lo_ref, j, diagonal=True):
    key = lax.broadcasted_iota(jnp.int32, (QT, KT), 1) + j * KT
    low = lo_ref[...]
    mask = key >= jnp.concatenate([low] * (KT // HD), axis=1)
    if diagonal:
        mask &= key <= lax.broadcasted_iota(jnp.int32, (QT, KT), 0) + W
    return mask


def masked(mask, x, other):
    return jnp.where(mask[None], x.reshape(2, QT, KT), other).reshape(2 * QT, KT)


def attend_clean(r0, groups, q_ref, k_ref, v_ref, o_ref, n_ref, range_ref):
    row = lax.broadcasted_iota(jnp.int32, (QT, KT), 0)
    col = lax.broadcasted_iota(jnp.int32, (QT, KT), 1)
    edge = col > row
    last = (TILES - 1) * KT
    weights = []
    for g in range(groups):
        s = scores_of(stacked_queries(q_ref, r0, g), k_ref, r0, g, TILES)
        ends = jnp.exp2(masked(edge, s[:, :KT], s[:, last:].reshape(2, QT, KT)) * SCALE2)
        middle = jnp.exp2(s[:, KT:last] * SCALE2)
        parts = [masked(edge, ends, 0.0), middle, masked(~edge, ends, 0.0)]
        weights.append(jnp.concatenate([x.astype(jnp.bfloat16) for x in parts], axis=1))
    for g in range(groups):
        finish(mix(weights[g], v_ref, r0, g, TILES), g, r0, o_ref, n_ref, range_ref)


def attend_masked(r0, j_lo, groups, q_ref, k_ref, v_ref, o_ref, n_ref, range_ref, lo_ref):
    count = TILES - j_lo
    row = pl.multiple_of(r0 + j_lo * KT, KT)
    weights = []
    for g in range(groups):
        s = scores_of(stacked_queries(q_ref, r0, g), k_ref, row, g, count)
        parts = []
        for j in range(count):
            p = jnp.exp2(s[:, j * KT : (j + 1) * KT] * SCALE2)
            mask = tile_mask(lo_ref, j_lo + j, j == count - 1)
            parts.append(masked(mask, p, 0.0).astype(jnp.bfloat16))
        weights.append(jnp.concatenate(parts, axis=1))
    for g in range(groups):
        finish(mix(weights[g], v_ref, row, g, count), g, r0, o_ref, n_ref, range_ref)


def attend_shifted(r0, j_lo, groups, q_ref, k_ref, v_ref, o_ref, n_ref, range_ref, lo_ref, acc_ref, top_ref):
    for g in range(groups):
        top_ref[...] = jnp.full_like(top_ref, -jnp.inf)
        acc_ref[g] = jnp.zeros_like(acc_ref[g])

        @pl.loop(j_lo, TILES)
        def _(j):
            row = pl.multiple_of(r0 + j * KT, KT)
            q2 = stacked_queries(q_ref, r0, g)
            s = masked(tile_mask(lo_ref, j), scores_of(q2, k_ref, row, g), -jnp.inf)
            top_ref[...] = jnp.maximum(top_ref[...], jnp.max(s, axis=1, keepdims=True))

        @pl.loop(j_lo, TILES)
        def _(j):
            row = pl.multiple_of(r0 + j * KT, KT)
            q2 = stacked_queries(q_ref, r0, g)
            top = jnp.concatenate([top_ref[...]] * (KT // HD), axis=1)
            p = jnp.exp2((scores_of(q2, k_ref, row, g) - top) * SCALE2)
            p = masked(tile_mask(lo_ref, j), p, 0.0)
            acc_ref[g] += mix(p.astype(jnp.bfloat16), v_ref, row, g)

        finish(acc_ref[g], g, r0, o_ref, n_ref, range_ref, top_ref[...])


def block_kernel(
    first_block, shard_rows, aliased, lengths_ref, live_ref, q_ref, k_ref, v_ref, *rest
):
    rest = rest[2:] if aliased else rest
    o_ref, n_ref, range_ref, lo_ref, acc_ref, top_ref = rest
    groups = k_ref.shape[1] // HD
    shard = lax.axis_index("ctx")
    block = pl.program_id(0) + first_block
    alive = block < live_ref[shard]
    block_start = shard * shard_rows + block * BLK

    @pl.when(jnp.logical_not(alive))
    def _():
        o_ref[...] = jnp.zeros_like(o_ref)
        n_ref[...] = jnp.zeros_like(n_ref)

    @pl.when(alive)
    def _():
        range_ref[0] = jnp.full((8, HD), TOTAL_HI, jnp.float32)
        range_ref[1] = jnp.full((8, HD), TOTAL_LO, jnp.float32)
        refs = (q_ref, k_ref, v_ref, o_ref, n_ref, range_ref)

        def low_tile(q0):
            reach = doc_start(lengths_ref, q0) - (q0 - W)
            return jnp.clip(reach // KT, 0, TILES - 1)

        @pl.loop(0, BLK // QT)
        def _(t):
            r0 = pl.multiple_of(t * QT, QT)
            q0 = block_start + r0
            clean = doc_start(lengths_ref, q0 + QT - 1) <= q0 - W + 1

            @pl.when(clean)
            def _():
                attend_clean(r0, groups, *refs)

            @pl.when(jnp.logical_not(clean))
            def _():
                set_low(lengths_ref, lo_ref, q0)
                first_tile = low_tile(q0)
                for j_lo in range(TILES):

                    @pl.when(first_tile == j_lo)
                    def _():
                        attend_masked(r0, j_lo, groups, *refs, lo_ref)

        in_range = (jnp.min(range_ref[0]) >= TOTAL_LO) & (jnp.max(range_ref[1]) <= TOTAL_HI)

        @pl.when(jnp.logical_not(in_range))
        def _():
            @pl.loop(0, BLK // QT)
            def _(t):
                r0 = pl.multiple_of(t * QT, QT)
                q0 = block_start + r0
                set_low(lengths_ref, lo_ref, q0)
                attend_shifted(r0, low_tile(q0), groups, *refs, lo_ref, acc_ref, top_ref)


def run_blocks(first_block, blocks, lengths, live, queries, keys, values, carried=None):
    shard_rows, width = queries.shape
    kv_width = keys.shape[1]
    heads = width // HD
    groups = kv_width // HD
    aliased = carried is not None

    def kernel(*refs):
        block_kernel(first_block, shard_rows, aliased, *refs)

    in_specs = [
        pl.BlockSpec((BLK, width), lambda i, *_: (i + first_block, 0)),
        pl.BlockSpec((pl.Element(SPAN), pl.Element(kv_width)), lambda i, *_: (i * BLK, 0)),
        pl.BlockSpec((pl.Element(SPAN), pl.Element(kv_width)), lambda i, *_: (i * BLK, 0)),
    ]
    if aliased:
        in_specs += [pl.BlockSpec(memory_space=pl.ANY)] * 2
    pairs = blocks * BLK * W * heads
    return pl.pallas_call(
        kernel,
        out_shape=(
            jax.ShapeDtypeStruct((shard_rows, width), jnp.bfloat16),
            jax.ShapeDtypeStruct((heads, shard_rows), jnp.float32),
        ),
        grid_spec=pltpu.PrefetchScalarGridSpec(
            num_scalar_prefetch=2,
            grid=(blocks,),
            in_specs=in_specs,
            out_specs=(
                pl.BlockSpec((BLK, width), lambda i, *_: (i + first_block, 0)),
                pl.BlockSpec((heads, BLK), lambda i, *_: (0, i + first_block)),
            ),
            scratch_shapes=[
                pltpu.VMEM((2, 8, HD), jnp.float32),
                pltpu.VMEM((QT, HD), jnp.int32),
                pltpu.VMEM((groups, 2 * QT, 2 * HD), jnp.float32),
                pltpu.VMEM((2 * QT, HD), jnp.float32),
            ],
        ),
        input_output_aliases={5: 0, 6: 1} if aliased else {},
        compiler_params=pltpu.CompilerParams(vmem_limit_bytes=48 << 20),
        cost_estimate=pl.CostEstimate(
            flops=4 * pairs * HD,
            transcendentals=pairs,
            bytes_accessed=blocks * (4 * BLK * width + 4 * SPAN * kv_width),
        ),
    )(lengths, live, queries, keys, values, *(carried or ()))


def local(queries, keys, values, doc_lengths, live_blocks):
    shard_rows = queries.shape[0]
    halo_blocks = W // BLK
    kv_width = keys.shape[1]
    tail = jnp.concatenate([keys[shard_rows - W :], values[shard_rows - W :]], axis=1)
    halo = from_behind(tail, "ctx", 1)
    done = run_blocks(
        halo_blocks, shard_rows // BLK - halo_blocks, doc_lengths, live_blocks, queries, keys, values
    )
    head_keys = jnp.concatenate([halo[:, :kv_width], keys[:W]], axis=0)
    head_values = jnp.concatenate([halo[:, kv_width:], values[:W]], axis=0)
    return run_blocks(
        0, halo_blocks, doc_lengths, live_blocks, queries, head_keys, head_values, done
    )


def solution(mesh):
    in_specs = (
        P(("groups", "ctx"), "head"),
        P(("groups", "ctx"), "head"),
        P(("groups", "ctx"), "head"),
        P("groups"),
        P("groups"),
    )
    out_specs = (P(("groups", "ctx"), "head"), P(("groups", "head"), "ctx"))
    return jax.shard_map(local, mesh=mesh, in_specs=in_specs, out_specs=out_specs, check_vma=False)
```

```python
import math

import jax
import jax.numpy as jnp
from jax import lax
from jax.experimental import pallas as pl
from jax.experimental.pallas import tpu as pltpu
from jax.sharding import PartitionSpec as P

HD = 128
W = 1024
BLK = 512
QT = 256
KT = 256
CT = 128
SPAN = W + BLK
TILES = (W + QT) // KT
SCALE = 168.0 ** (-0.5)
SCALE2 = SCALE * math.log2(math.e)
TOTAL_LO = 2.0 ** -40
TOTAL_HI = 2.0 ** 100


def from_behind(shard, axis, by):
    devices = lax.axis_size(axis)
    pairs = [(i, i + by) for i in range(devices) if 0 <= i + by < devices]
    return lax.ppermute(shard, axis, pairs)


def doc_start(lengths_ref, position):
    start = jnp.int32(0)
    found = jnp.int32(0)
    for n in range(lengths_ref.shape[0]):
        found = jnp.where(start <= position, start, found)
        start = start + lengths_ref[n]
    return found


def scores_of(q2, k_ref, row, g, keys=KT):
    k = k_ref[pl.ds(row, keys), g * HD : (g + 1) * HD]
    return lax.dot_general(q2, k, (((1,), (1,)), ((), ())), preferred_element_type=jnp.float32)


def mix(p, v_ref, row, g, keys=KT):
    v = v_ref[pl.ds(row, keys), g * HD : (g + 1) * HD]
    v_ones = jnp.concatenate([v, jnp.ones((keys, HD), v.dtype)], axis=1)
    return jnp.dot(p, v_ones, preferred_element_type=jnp.float32)


def stacked_queries(q_ref, r0, g, rows=QT):
    a = q_ref[pl.ds(r0, rows), 2 * g * HD : (2 * g + 1) * HD]
    b = q_ref[pl.ds(r0, rows), (2 * g + 1) * HD : (2 * g + 2) * HD]
    return jnp.concatenate([a, b], axis=0)


def lane_row(x):
    at = (HD, HD)
    own = lax.broadcasted_iota(jnp.int32, at, 0) == lax.broadcasted_iota(jnp.int32, at, 1)
    parts = [
        jnp.sum(jnp.where(own, x[i : i + HD], 0.0), axis=0, keepdims=True)
        for i in range(0, x.shape[0], HD)
    ]
    return jnp.concatenate(parts, axis=1)


def finish(acc, g, r0, o_ref, n_ref, range_ref, top=None):
    rows = acc.shape[0] // 2
    total = acc[:, HD:]
    out = (acc[:, :HD] / total).astype(o_ref.dtype)
    for h in range(2):
        col = (2 * g + h) * HD
        o_ref[pl.ds(r0, rows), col : col + HD] = out[h * rows : (h + 1) * rows]
        row = jnp.log(lane_row(total[h * rows : (h + 1) * rows]))
        if top is not None:
            row = row + lane_row(top[h * rows : (h + 1) * rows]) * SCALE
        n_ref[2 * g + h : 2 * g + h + 1, pl.ds(r0, rows)] = row
    if top is None:
        folded = total.reshape(2 * rows // 8, 8, HD)
        range_ref[0] = jnp.minimum(range_ref[0], jnp.min(folded, axis=0))
        range_ref[1] = jnp.maximum(range_ref[1], jnp.max(folded, axis=0))


def set_low(lengths_ref, lo_ref, q0):
    q = lax.broadcasted_iota(jnp.int32, (QT, HD), 0)
    low = q + 1
    start = jnp.int32(0)
    first = q0 - W
    lo_ref[...] = low
    for n in range(lengths_ref.shape[0]):
        here = start

        @pl.when((here > first) & (here < q0 + QT))
        def _():
            rel = here - first
            at = lax.broadcasted_iota(jnp.int32, (QT, HD), 0) + W
            lo_ref[...] = jnp.where(at >= rel, jnp.maximum(lo_ref[...], rel), lo_ref[...])

        start = start + lengths_ref[n]


def tile_mask(lo_ref, j, diagonal=True):
    key = lax.broadcasted_iota(jnp.int32, (QT, KT), 1) + j * KT
    low = lo_ref[...]
    mask = key >= jnp.concatenate([low] * (KT // HD), axis=1)
    if diagonal:
        mask &= key <= lax.broadcasted_iota(jnp.int32, (QT, KT), 0) + W
    return mask


def masked(mask, x, other):
    return jnp.where(mask[None], x.reshape(2, *mask.shape), other).reshape(x.shape)


def attend_clean(starts, groups, q_ref, k_ref, v_ref, o_ref, n_ref, range_ref):
    row = lax.broadcasted_iota(jnp.int32, (CT, CT), 0)
    col = lax.broadcasted_iota(jnp.int32, (CT, CT), 1)
    edge = col > row
    chains = [(r0, g) for r0 in starts for g in range(groups)]
    weights = []
    for r0, g in chains:
        s = scores_of(stacked_queries(q_ref, r0, g, CT), k_ref, r0, g, W + CT)
        ends = jnp.exp2(masked(edge, s[:, :CT], s[:, W:].reshape(2, CT, CT)) * SCALE2)
        middle = jnp.exp2(s[:, CT:W] * SCALE2)
        parts = [masked(edge, ends, 0.0), middle, masked(~edge, ends, 0.0)]
        weights.append(jnp.concatenate([x.astype(jnp.bfloat16) for x in parts], axis=1))
    for (r0, g), p in zip(chains, weights):
        finish(mix(p, v_ref, r0, g, W + CT), g, r0, o_ref, n_ref, range_ref)


def attend_masked(r0, j_lo, groups, q_ref, k_ref, v_ref, o_ref, n_ref, range_ref, lo_ref):
    count = TILES - j_lo
    row = pl.multiple_of(r0 + j_lo * KT, KT)
    weights = []
    for g in range(groups):
        s = scores_of(stacked_queries(q_ref, r0, g), k_ref, row, g, count * KT)
        parts = []
        for j in range(count):
            p = jnp.exp2(s[:, j * KT : (j + 1) * KT] * SCALE2)
            mask = tile_mask(lo_ref, j_lo + j, j == count - 1)
            parts.append(masked(mask, p, 0.0).astype(jnp.bfloat16))
        weights.append(jnp.concatenate(parts, axis=1))
    for g in range(groups):
        finish(mix(weights[g], v_ref, row, g, count * KT), g, r0, o_ref, n_ref, range_ref)


def attend_shifted(r0, j_lo, groups, q_ref, k_ref, v_ref, o_ref, n_ref, range_ref, lo_ref, acc_ref, top_ref):
    for g in range(groups):
        top_ref[...] = jnp.full_like(top_ref, -jnp.inf)
        acc_ref[g] = jnp.zeros_like(acc_ref[g])

        @pl.loop(j_lo, TILES)
        def _(j):
            row = pl.multiple_of(r0 + j * KT, KT)
            q2 = stacked_queries(q_ref, r0, g)
            s = masked(tile_mask(lo_ref, j), scores_of(q2, k_ref, row, g), -jnp.inf)
            top_ref[...] = jnp.maximum(top_ref[...], jnp.max(s, axis=1, keepdims=True))

        @pl.loop(j_lo, TILES)
        def _(j):
            row = pl.multiple_of(r0 + j * KT, KT)
            q2 = stacked_queries(q_ref, r0, g)
            top = jnp.concatenate([top_ref[...]] * (KT // HD), axis=1)
            p = jnp.exp2((scores_of(q2, k_ref, row, g) - top) * SCALE2)
            p = masked(tile_mask(lo_ref, j), p, 0.0)
            acc_ref[g] += mix(p.astype(jnp.bfloat16), v_ref, row, g)

        finish(acc_ref[g], g, r0, o_ref, n_ref, range_ref, top_ref[...])


def block_kernel(
    first_block, shard_rows, aliased, lengths_ref, live_ref, q_ref, k_ref, v_ref, *rest
):
    rest = rest[2:] if aliased else rest
    o_ref, n_ref, range_ref, lo_ref, acc_ref, top_ref = rest
    groups = k_ref.shape[1] // HD
    shard = lax.axis_index("ctx")
    block = pl.program_id(0) + first_block
    alive = block < live_ref[shard]
    block_start = shard * shard_rows + block * BLK

    @pl.when(jnp.logical_not(alive))
    def _():
        o_ref[...] = jnp.zeros_like(o_ref)
        n_ref[...] = jnp.zeros_like(n_ref)

    @pl.when(alive)
    def _():
        range_ref[0] = jnp.full((8, HD), TOTAL_HI, jnp.float32)
        range_ref[1] = jnp.full((8, HD), TOTAL_LO, jnp.float32)
        refs = (q_ref, k_ref, v_ref, o_ref, n_ref, range_ref)

        def low_tile(q0):
            reach = doc_start(lengths_ref, q0) - (q0 - W)
            return jnp.clip(reach // KT, 0, TILES - 1)

        clean_block = doc_start(lengths_ref, block_start + BLK - 1) <= block_start - W + 1

        @pl.when(clean_block)
        def _():
            attend_clean(range(0, BLK, CT), groups, *refs)

        @pl.loop(0, jnp.where(clean_block, 0, BLK // QT))
        def _(t):
            r0 = pl.multiple_of(t * QT, QT)
            q0 = block_start + r0
            clean = doc_start(lengths_ref, q0 + QT - 1) <= q0 - W + 1

            @pl.when(clean)
            def _():
                attend_clean([r0 + n for n in range(0, QT, CT)], groups, *refs)

            @pl.when(jnp.logical_not(clean))
            def _():
                set_low(lengths_ref, lo_ref, q0)
                first_tile = low_tile(q0)
                for j_lo in range(TILES):

                    @pl.when(first_tile == j_lo)
                    def _():
                        attend_masked(r0, j_lo, groups, *refs, lo_ref)

        in_range = (jnp.min(range_ref[0]) >= TOTAL_LO) & (jnp.max(range_ref[1]) <= TOTAL_HI)

        @pl.when(jnp.logical_not(in_range))
        def _():
            @pl.loop(0, BLK // QT)
            def _(t):
                r0 = pl.multiple_of(t * QT, QT)
                q0 = block_start + r0
                set_low(lengths_ref, lo_ref, q0)
                attend_shifted(r0, low_tile(q0), groups, *refs, lo_ref, acc_ref, top_ref)


def run_blocks(first_block, blocks, lengths, live, queries, keys, values, carried=None):
    shard_rows, width = queries.shape
    kv_width = keys.shape[1]
    heads = width // HD
    groups = kv_width // HD
    aliased = carried is not None

    def kernel(*refs):
        block_kernel(first_block, shard_rows, aliased, *refs)

    in_specs = [
        pl.BlockSpec((BLK, width), lambda i, *_: (i + first_block, 0)),
        pl.BlockSpec((pl.Element(SPAN), pl.Element(kv_width)), lambda i, *_: (i * BLK, 0)),
        pl.BlockSpec((pl.Element(SPAN), pl.Element(kv_width)), lambda i, *_: (i * BLK, 0)),
    ]
    if aliased:
        in_specs += [pl.BlockSpec(memory_space=pl.ANY)] * 2
    pairs = blocks * BLK * W * heads
    return pl.pallas_call(
        kernel,
        out_shape=(
            jax.ShapeDtypeStruct((shard_rows, width), jnp.bfloat16),
            jax.ShapeDtypeStruct((heads, shard_rows), jnp.float32),
        ),
        grid_spec=pltpu.PrefetchScalarGridSpec(
            num_scalar_prefetch=2,
            grid=(blocks,),
            in_specs=in_specs,
            out_specs=(
                pl.BlockSpec((BLK, width), lambda i, *_: (i + first_block, 0)),
                pl.BlockSpec((heads, BLK), lambda i, *_: (0, i + first_block)),
            ),
            scratch_shapes=[
                pltpu.VMEM((2, 8, HD), jnp.float32),
                pltpu.VMEM((QT, HD), jnp.int32),
                pltpu.VMEM((groups, 2 * QT, 2 * HD), jnp.float32),
                pltpu.VMEM((2 * QT, HD), jnp.float32),
            ],
        ),
        input_output_aliases={5: 0, 6: 1} if aliased else {},
        compiler_params=pltpu.CompilerParams(vmem_limit_bytes=48 << 20),
        cost_estimate=pl.CostEstimate(
            flops=4 * pairs * HD,
            transcendentals=pairs,
            bytes_accessed=blocks * (4 * BLK * width + 4 * SPAN * kv_width),
        ),
    )(lengths, live, queries, keys, values, *(carried or ()))


def local(queries, keys, values, doc_lengths, live_blocks):
    shard_rows = queries.shape[0]
    halo_blocks = W // BLK
    kv_width = keys.shape[1]
    tail = jnp.concatenate([keys[shard_rows - W :], values[shard_rows - W :]], axis=1)
    halo = from_behind(tail, "ctx", 1)
    done = run_blocks(
        halo_blocks, shard_rows // BLK - halo_blocks, doc_lengths, live_blocks, queries, keys, values
    )
    head_keys = jnp.concatenate([halo[:, :kv_width], keys[:W]], axis=0)
    head_values = jnp.concatenate([halo[:, kv_width:], values[:W]], axis=0)
    return run_blocks(
        0, halo_blocks, doc_lengths, live_blocks, queries, head_keys, head_values, done
    )


def solution(mesh):
    in_specs = (
        P(("groups", "ctx"), "head"),
        P(("groups", "ctx"), "head"),
        P(("groups", "ctx"), "head"),
        P("groups"),
        P("groups"),
    )
    out_specs = (P(("groups", "ctx"), "head"), P(("groups", "head"), "ctx"))
    return jax.shard_map(local, mesh=mesh, in_specs=in_specs, out_specs=out_specs, check_vma=False)
```
